32 devices in a mesh: hel: 4 (over z), rad: 8 (over y, x, core).
Axes of the slice: x: 2, y: 2, z: 4, core: 2. Of those that a mesh axis runs over, the one named last changes fastest.
Arguments:
- packet: float32 [2, 8, 1024, 8, 1024], P(None, 'hel', 'rad'), may hold values from -6 to 6
- radial_weight: float32 [8, 1024], P(None, 'rad'), may hold values from 0.25 to 1.75
- tile_blocks: float32 [24, 128, 128], replicated, may hold values from -0.1875 to 0.1875
- tile_list: int32 [24, 3], replicated, may hold values from 0 to 7, as said below
- coupling: float32 [8, 1024], replicated, may hold values from 0.1 to 0.5
Outputs:
- advanced: float32 [2, 8, 1024, 8, 1024], P(None, 'hel', 'rad')
The draws below stay inside these ranges and needn't reach their ends.
Inputs may be any that keep to these rules, and one draw needn't show every extreme that they name: `tile_list`: each row is (block row, block column, radial weight index): block indices lie below 8 and weight indices below 8; every block row and every weight index occurs in some row; rows may repeat pairs.
All inputs are finite; a program needn't handle non-finite values.
Results may differ from the reference program's by a relative error of at most 0.0001.
Values sent between devices are 32-bit elements; how exact they have to be, the bound alone decides.
No kernel may reach another device: no remote copies, remote signals or barrier semaphores. Data moves between devices by JAX's collectives and lax.ppermute only.
A program may use at most 256 MiB of HBM per device.

```python
import jax
import jax.numpy as jnp
from jax import lax

K = 8
V = 8
R = 1024
C = 1024
TILE = 128
NT = 24
Q = 8
TAYLOR = 3


def draw_tile_list(key, part):
    key_rows, key_cols, key_weights, key_pick_rows, key_pick_weights = jax.random.split(jax.random.fold_in(key, 17), 5)
    block_count = C // TILE
    rows_drawn = jax.random.randint(key_rows, (NT,), 0, block_count)
    chosen_rows = jax.random.permutation(key_pick_rows, NT)[:block_count]
    rows_drawn = rows_drawn.at[chosen_rows].set(jnp.arange(block_count, dtype=jnp.int32))
    cols_drawn = jax.random.randint(key_cols, (NT,), 0, block_count)
    weights_drawn = jax.random.randint(key_weights, (NT,), 0, Q)
    chosen_weights = jax.random.permutation(key_pick_weights, NT)[:Q]
    weights_drawn = weights_drawn.at[chosen_weights].set(jnp.arange(Q, dtype=jnp.int32))
    return jnp.stack([rows_drawn, cols_drawn, weights_drawn], axis=1).astype(jnp.int32)


def block_levels(own_key, extent, cuts, smallest, top_value):
    loudness = 1.0
    for axis_at, shards_of in cuts:
        draws = jax.random.uniform(jax.random.fold_in(jax.random.fold_in(own_key, 6), axis_at), (shards_of,), jnp.float32, smallest / len(cuts), top_value / len(cuts))
        loudness = loudness * jnp.repeat(jnp.exp(draws), extent[axis_at] // shards_of).reshape((-1,) + (1,) * (len(extent) - 1 - axis_at))
    return loudness


def scatter_about(own_key, extent, width, reach, pieces=(), kind=jnp.bfloat16):
    entries = jax.random.normal(own_key, extent, jnp.float32) * width
    if len(pieces) > 0:
        entries = block_levels(own_key, extent, pieces, -0.22, 0.18) * entries
    return jnp.clip(entries, min=-reach, max=reach).astype(kind)


def setup_inputs(seed: int = 0) -> dict:
    key_list = jax.random.split(jax.random.key(seed), 6)
    packet = scatter_about(key_list[0], (2, K, R, V, C), 1.0, 6.0, ((1, 4), (2, 8)), jnp.float32)
    radial_weight = jnp.clip(0.25 + 1.5 * jax.random.uniform(key_list[1], (Q, R), jnp.float32) ** block_levels(key_list[1], (Q, R), ((1, 8),), -0.2, 0.2), 0.25, 1.75)
    tile_blocks = scatter_about(key_list[2], (NT, TILE, TILE), (3 * TILE * NT * TILE // C) ** -0.5, 0.1875, (), jnp.float32)
    tile_list = draw_tile_list(jax.random.fold_in(key_list[5], 71), 0)
    coupling = jnp.clip(jax.random.uniform(key_list[4], (K, C), jnp.float32, 0.1, 0.5), 0.1, 0.5)
    return {"packet": packet, "radial_weight": radial_weight, "tile_blocks": tile_blocks, "tile_list": tile_list, "coupling": coupling}


kinetic_scale = 0.5


def potential(term, radial_weight, tile_blocks, tile_list):
    term_shape = term.shape
    blocks = term.reshape(term_shape[0], term_shape[1], term_shape[2], term_shape[3], term_shape[4] // TILE, TILE)

    def add_tile(position, summed):
        target = tile_list[position, 0]
        source = tile_list[position, 1]
        weight_row = tile_list[position, 2]
        source_block = lax.dynamic_index_in_dim(blocks, source, 4, keepdims=False)
        matrix = lax.dynamic_index_in_dim(tile_blocks, position, 0, keepdims=False)
        product = jnp.einsum("ckrvi,ij->ckrvj", source_block, matrix, precision=lax.Precision.HIGHEST)
        factor = lax.dynamic_index_in_dim(radial_weight, weight_row, 0, keepdims=False)
        product = product * factor[None, None, :, None, None]
        current = lax.dynamic_index_in_dim(summed, target, 4, keepdims=False)
        return lax.dynamic_update_index_in_dim(summed, current + product, target, 4)

    summed = lax.fori_loop(0, tile_list.shape[0], add_tile, jnp.zeros(blocks.shape, jnp.float32))
    return summed.reshape(term_shape)


def coriolis(term, coupling, radial_factor):
    helices = term.shape[1]
    padded = jnp.pad(term, ((0, 0), (1, 1), (0, 0), (0, 0), (0, 0)))
    coupled = jnp.concatenate([jnp.zeros((1, coupling.shape[1]), jnp.float32), coupling], axis=0)
    lower = coupled[:helices]
    upper = coupled[1:helices + 1]
    mixed = upper[None, :, None, None, :] * padded[:, 2:] + lower[None, :, None, None, :] * padded[:, :-2]
    return mixed * radial_factor[None, None, :, None, None]


def kinetic(packet):
    wave_index = jnp.arange(R, dtype=jnp.int32)
    signed = jnp.where(wave_index < R // 2, wave_index, wave_index - R).astype(jnp.float32)
    phase_angle = kinetic_scale * (2.0 * jnp.pi * signed / R) ** 2
    complex_field = packet[0] + 1j * packet[1]
    spectrum = jnp.fft.fft(complex_field, axis=1) * jnp.exp(-1j * phase_angle)[None, :, None, None]
    complex_field = jnp.fft.ifft(spectrum, axis=1)
    return jnp.stack([jnp.real(complex_field), jnp.imag(complex_field)]).astype(packet.dtype)


def reference(packet, radial_weight, tile_blocks, tile_list, coupling):
    distance = jnp.arange(R).astype(jnp.float32)
    radial_factor = 1.0 / (1.0 + 3.0 * distance / R) ** 2
    current = kinetic(packet)
    advanced = current
    for degree in range(1, TAYLOR + 1):
        applied = potential(current, radial_weight, tile_blocks, tile_list) + coriolis(current, coupling, radial_factor)
        current = jnp.stack([applied[1], -applied[0]]) / degree
        advanced = advanced + current
    return advanced
```

```python
import functools

import jax
import jax.numpy as jnp
import numpy as np
from jax import lax
from jax.experimental import pallas as pl
from jax.experimental.pallas import tpu as pltpu
from jax.sharding import PartitionSpec as P


R = 1024
TILE = 128
TAYLOR = 3
CHUNKS = (2, 1, 2, 2, 1)
EARLY = (4,)
PLAN = (
    ("F", 0), ("F", 1), ("K", 0), ("B", 0), ("K", 1), ("B", 1), ("E", 0), ("F", 2), ("E", 1),
    ("T", 0), ("K", 2), ("B", 2), ("T", 1), ("T", 0), ("F", 3), ("E", 2), ("T", 1), ("F", 4),
    ("K", 3), ("B", 3), ("T", 2), ("T", 1), ("K", 4), ("B", 4), ("E", 3), ("T", 2), ("G", 4),
    ("T", 3), ("L", 4), ("C", 4), ("T", 0), ("T", 2), ("T", 4), ("T", 3), ("T", 4), ("T", 3),
    ("T", 4),
)


kinetic_scale = 0.5


def extended(block, sides, width):
    for axis, dim in sides:
        count = lax.axis_size(axis)
        forward = [(i, i + 1) for i in range(count - 1)]
        backward = [(target, source) for source, target in forward]
        low = lax.ppermute(
            lax.slice_in_dim(block, block.shape[dim] - width, None, axis=dim), axis, forward
        )
        high = lax.ppermute(lax.slice_in_dim(block, 0, width, axis=dim), axis, backward)
        block = jnp.concatenate([low, block, high], axis=dim)
    return block


def potential(term, radial_weight, tile_blocks, tile_list):
    term_shape = term.shape
    blocks = term.reshape(
        term_shape[0], term_shape[1], term_shape[2], term_shape[3], term_shape[4] // TILE, TILE
    )

    def add_tile(position, summed):
        target = tile_list[position, 0]
        source = tile_list[position, 1]
        weight_row = tile_list[position, 2]
        source_block = lax.dynamic_index_in_dim(blocks, source, 4, keepdims=False)
        matrix = lax.dynamic_index_in_dim(tile_blocks, position, 0, keepdims=False)
        product = jnp.einsum(
            "ckrvi,ij->ckrvj", source_block, matrix, precision=lax.Precision.HIGHEST
        )
        factor = lax.dynamic_index_in_dim(radial_weight, weight_row, 0, keepdims=False)
        product = product * factor[None, None, :, None, None]
        current = lax.dynamic_index_in_dim(summed, target, 4, keepdims=False)
        return lax.dynamic_update_index_in_dim(summed, current + product, target, 4)

    summed = lax.fori_loop(0, tile_list.shape[0], add_tile, jnp.zeros(blocks.shape, jnp.float32))
    return summed.reshape(term_shape)


def coupling_window(coupling, helices):
    first_helix = lax.axis_index("hel") * helices
    coupled = jnp.concatenate([jnp.zeros((1, coupling.shape[1]), jnp.float32), coupling], axis=0)
    return lax.dynamic_slice_in_dim(coupled, first_helix, helices + 1, 0)


def coriolis_rim(term, coupling, radial_factor):
    helices = term.shape[1]
    padded = extended(term, (("hel", 1),), 1)
    window = coupling_window(coupling, helices)
    lower = window[:helices]
    upper = window[1:]
    mixed = (
        upper[None, :, None, None, :] * padded[:, 2:]
        + lower[None, :, None, None, :] * padded[:, :-2]
    )
    return mixed * radial_factor[None, None, :, None, None]


def transform(matrix, moving):
    return jnp.einsum("qr,cnrm->cnqm", matrix, moving, precision=lax.Precision.HIGHEST)


def propagate(moving, cosine_table, sine_table, phase_cos, phase_sin):
    length = moving.shape[2]
    cos_part = transform(cosine_table, moving)
    sin_part = transform(sine_table, moving)
    spec_real = cos_part[0] + sin_part[1]
    spec_imag = cos_part[1] - sin_part[0]
    turn_cos = phase_cos[None, :, None]
    turn_sin = phase_sin[None, :, None]
    turned = jnp.stack(
        [turn_cos * spec_real + turn_sin * spec_imag, turn_cos * spec_imag - turn_sin * spec_real]
    )
    cos_back = transform(cosine_table, turned)
    sin_back = transform(sine_table, turned)
    return jnp.stack([(cos_back[0] - sin_back[1]) / length, (cos_back[1] + sin_back[0]) / length])


def expand(current, radial_weight, tile_blocks, tile_list, coupling, radial_factor, coriolis):
    advanced = current
    for degree in range(1, TAYLOR + 1):
        applied = potential(current, radial_weight, tile_blocks, tile_list) + coriolis(
            current, coupling, radial_factor
        )
        current = jnp.stack([applied[1], -applied[0]]) / degree
        advanced = advanced + current
    return advanced


def radial_factor_of(radial):
    distance = (lax.axis_index("rad") * radial + jnp.arange(radial, dtype=jnp.int32)).astype(
        jnp.float32
    )
    return 1.0 / (1.0 + 3.0 * distance / R) ** 2


def body_any(packet, radial_weight, tile_blocks, tile_list, coupling):
    two_parts, helices, radial, vibration, channels = packet.shape
    wave_index = jnp.arange(R, dtype=jnp.int32)
    angle_table = (wave_index[:, None] * wave_index[None, :] % R).astype(jnp.float32) * (
        2.0 * jnp.pi / R
    )
    cosine_table = jnp.cos(angle_table)
    sine_table = jnp.sin(angle_table)
    signed = jnp.where(wave_index < R // 2, wave_index, wave_index - R).astype(jnp.float32)
    phase_angle = kinetic_scale * (2.0 * jnp.pi * signed / R) ** 2
    phase_cos = jnp.cos(phase_angle)
    phase_sin = jnp.sin(phase_angle)
    flattened = packet.reshape(two_parts, helices, radial, vibration * channels)
    moved = propagate(
        lax.all_to_all(flattened, "rad", split_axis=3, concat_axis=2, tiled=True),
        cosine_table,
        sine_table,
        phase_cos,
        phase_sin,
    )
    returned = lax.all_to_all(moved, "rad", split_axis=2, concat_axis=3, tiled=True)
    current = returned.reshape(packet.shape)
    return expand(
        current,
        radial_weight,
        tile_blocks,
        tile_list,
        coupling,
        radial_factor_of(radial),
        coriolis_rim,
    )


VMEM_LIMIT = 60 * 1024 * 1024


def params(axes):
    return pltpu.CompilerParams(
        dimension_semantics=("arbitrary",) * axes, vmem_limit_bytes=VMEM_LIMIT
    )


def split_two(value):
    high = value.astype(jnp.bfloat16)
    low = (value - high.astype(jnp.float32)).astype(jnp.bfloat16)
    return high, low


def propagator_column(length):
    wave = np.arange(length)
    signed = np.where(wave < length // 2, wave, wave - length).astype(np.float64)
    phase = kinetic_scale * (2.0 * np.pi * signed / length) ** 2
    column = np.fft.ifft(np.exp(-1j * phase))
    return column.real.astype(np.float32), column.imag.astype(np.float32)


STRIPE = 16
ROWS = 64
UNROLL = 8


def circulant_kernel(real_ref, imag_ref, high_ref, low_ref):
    rows = high_ref.shape[2]
    first = pl.program_id(0) * rows
    for part, ref in ((0, real_ref), (1, imag_ref)):
        stripe = jnp.broadcast_to(ref[...], (STRIPE, ref.shape[1]))
        row = lax.broadcasted_iota(jnp.int32, stripe.shape, 0)
        step = 1
        while step < STRIPE:
            stripe = jnp.where(row // step % 2 == 1, pltpu.roll(stripe, step, 1), stripe)
            step *= 2

        @pl.loop(0, rows // STRIPE)
        def _(j):
            at = pl.multiple_of(j * STRIPE, STRIPE)
            high, low = split_two(pltpu.roll(stripe, first + at, 1))
            high_ref[0, part, pl.ds(at, STRIPE)] = high
            low_ref[0, part, pl.ds(at, STRIPE)] = low


def circulant(length, rows):
    real, imag = propagator_column(length)
    grid = length // rows
    spec = pl.BlockSpec((1, 2, rows, length), lambda m: (m, 0, 0, 0))
    line = pl.BlockSpec((1, length), lambda m: (0, 0))
    shape = jax.ShapeDtypeStruct((grid, 2, rows, length), jnp.bfloat16)
    return pl.pallas_call(
        circulant_kernel,
        grid=(grid,),
        in_specs=[line, line],
        out_specs=[spec, spec],
        out_shape=[shape, shape],
        compiler_params=params(1),
        name="circulant",
    )(jnp.asarray(real)[None], jnp.asarray(imag)[None])


def kinetic_kernel(*refs):
    moving_ref, high_ref, low_ref, out_ref, xh_ref, xl_ref = refs[-6:]
    sources, _, _, _, radial, lanes = moving_ref.shape
    length = sources * radial
    for part in range(2):
        value = moving_ref[:, 0, 0, part].reshape(length, lanes)
        high, low = split_two(value)
        xh_ref[:, part * lanes : (part + 1) * lanes] = high
        xl_ref[:, part * lanes : (part + 1) * lanes] = low
    groups, _, rows, _ = high_ref.shape
    per = rows // radial

    @pl.loop(0, groups, unroll=2)
    def _(m):
        left = high_ref[m].reshape(2 * rows, length)
        small = low_ref[m].reshape(2 * rows, length)
        dot = functools.partial(jnp.dot, preferred_element_type=jnp.float32)
        high = xh_ref[...]
        total = dot(left, high) + (dot(left, xl_ref[...]) + dot(small, high))
        real = total[:rows, :lanes] - total[rows:, lanes:]
        imag = total[:rows, lanes:] + total[rows:, :lanes]
        for j in range(per):
            out_ref[m * per + j, 0, 0, 0] = real[j * radial : (j + 1) * radial]
            out_ref[m * per + j, 0, 0, 1] = imag[j * radial : (j + 1) * radial]


def kinetic(moving, high, low, afters):
    blocks, helices, count, _, radial, lanes = moving.shape
    block = pl.BlockSpec((blocks, 1, 1, 2, radial, lanes), lambda k, v: (0, k, v, 0, 0, 0))
    whole = pl.BlockSpec(high.shape, lambda k, v: (0, 0, 0, 0), pipeline_mode=pl.Buffered(1))
    length = blocks * radial
    return pl.pallas_call(
        kinetic_kernel,
        grid=(helices, count),
        in_specs=[*[ANYWHERE] * len(afters), block, whole, whole],
        out_specs=block,
        out_shape=jax.ShapeDtypeStruct(moving.shape, jnp.float32),
        scratch_shapes=[
            pltpu.VMEM((length, 2 * lanes), jnp.bfloat16),
            pltpu.VMEM((length, 2 * lanes), jnp.bfloat16),
        ],
        compiler_params=params(2),
        cost_estimate=pl.CostEstimate(
            flops=2 * 3 * helices * count * 4 * length * length * lanes,
            bytes_accessed=8 * moving.size + 8 * length * length,
            transcendentals=0,
        ),
        name="kinetic",
    )(*afters, moving, high, low)


def places():
    return [(c, i) for c, count in enumerate(CHUNKS) for i in range(count)]


def pack_kernel(chunks, packet_ref, *chunk_refs):
    @pl.loop(0, packet_ref.shape[4] // TILE)
    def _(b):
        lanes = pl.ds(pl.multiple_of(b * TILE, TILE), TILE)
        turned = jnp.swapaxes(packet_ref[0, 0, :, :, lanes], 0, 1)
        for v, (c, i) in enumerate(places()):
            if c in chunks:
                chunk_refs[chunks.index(c)][b, 0, i, 0] = turned[v]


def pack(packet, chunks):
    parts, helices, radial, vibration, channels = packet.shape
    blocks = channels // TILE
    counts = [CHUNKS[c] for c in chunks]
    share = sum(counts) / vibration
    return pl.pallas_call(
        functools.partial(pack_kernel, chunks),
        grid=(helices, parts),
        in_specs=[
            pl.BlockSpec((1, 1, radial, vibration, channels), lambda k, p: (p, k, 0, 0, 0))
        ],
        out_specs=[
            pl.BlockSpec((blocks, 1, count, 1, radial, TILE), lambda k, p: (0, k, 0, p, 0, 0))
            for count in counts
        ],
        out_shape=[
            jax.ShapeDtypeStruct((blocks, helices, count, parts, radial, TILE), jnp.float32)
            for count in counts
        ],
        compiler_params=params(2),
        cost_estimate=pl.CostEstimate(
            flops=0, bytes_accessed=int(4 * packet.size * (1 + share)), transcendentals=0
        ),
        name="pack",
    )(packet)


def unpack_kernel(*refs):
    out_ref = refs[-1]

    @pl.loop(0, out_ref.shape[4] // TILE)
    def _(b):
        lanes = pl.ds(pl.multiple_of(b * TILE, TILE), TILE)
        lines = [refs[c][0, b, i, 0] for c, i in places()]
        out_ref[0, 0, :, :, lanes] = jnp.swapaxes(jnp.stack(lines), 0, 1)


def unpack(chunks, packet_shape):
    parts, helices, radial, vibration, channels = packet_shape
    blocks = channels // TILE
    return pl.pallas_call(
        unpack_kernel,
        grid=(helices, parts),
        in_specs=[
            pl.BlockSpec((1, blocks, count, 1, radial, TILE), lambda k, p: (k, 0, 0, p, 0, 0))
            for count in CHUNKS
        ],
        out_specs=pl.BlockSpec(
            (1, 1, radial, vibration, channels), lambda k, p: (p, k, 0, 0, 0)
        ),
        out_shape=jax.ShapeDtypeStruct(packet_shape, jnp.float32),
        compiler_params=params(2),
        name="unpack",
    )(*chunks)


def gate_kernel(*refs):
    del refs


ANYWHERE = pl.BlockSpec(memory_space=pl.ANY)


def gate(value, *afters):
    return pl.pallas_call(
        gate_kernel,
        in_specs=[ANYWHERE] * (1 + len(afters)),
        out_specs=ANYWHERE,
        out_shape=jax.ShapeDtypeStruct(value.shape, value.dtype),
        input_output_aliases={0: 0},
        compiler_params=params(0),
        name="gate",
    )(value, *afters)


def taylor_kernel(degree, helices, skipped, sums_in, last, list_ref, *refs):
    refs = list(refs)[skipped:]
    term_refs = [refs.pop(0) for _ in range(helices)]
    low_ref, high_ref, tile_ref, weight_ref, window_ref, factor_ref = (
        refs.pop(0) for _ in range(6)
    )
    sum_refs = [refs.pop(0) for _ in range(helices)] if sums_in else []
    next_refs = None if last else [refs.pop(0) for _ in range(helices)]
    total_refs = [refs.pop(0) for _ in range(helices)] if sums_in and not last else None
    out_ref = refs.pop(0) if last else None
    split_ref, summed_ref = refs
    term_refs, sum_refs, (low_ref, high_ref) = (
        [r.at[:, 0] if len(r.shape) == 6 else r for r in some]
        for some in (term_refs, sum_refs, (low_ref, high_ref))
    )
    blocks, _, _, radial, lanes = term_refs[0].shape
    rows = helices * 2 * radial
    factor = factor_ref[...]

    @pl.loop(0, blocks)
    def _(b):
        for k in range(helices):
            below = low_ref if k == 0 else term_refs[k - 1]
            above = high_ref if k == helices - 1 else term_refs[k + 1]
            lower = window_ref[k, b]
            upper = window_ref[k + 1, b]
            for part in range(2):
                at = (k * 2 + part) * radial
                high, low = split_two(term_refs[k][b, 0, part])
                split_ref[b, at : at + radial, :lanes] = high
                split_ref[b, at : at + radial, lanes:] = low
                mixed = upper * above[b, 0, part] + lower * below[b, 0, part]
                summed_ref[b, at : at + radial] = mixed * factor

    def add_tile(t, carry):
        target = list_ref[t, 0]
        source = list_ref[t, 1]
        weight = weight_ref[list_ref[t, 2]]
        both = jnp.dot(split_ref[source], tile_ref[t], preferred_element_type=jnp.float32)
        for i in range(rows // radial):
            at = i * radial
            product = both[at : at + radial, :lanes] + both[at : at + radial, lanes:]
            summed_ref[target, at : at + radial] += product * weight
        return carry

    lax.fori_loop(0, tile_ref.shape[0], add_tile, 0, unroll=UNROLL)

    scale = 1.0 / degree

    @pl.loop(0, blocks)
    def _(b):
        for k in range(helices):
            at = k * 2 * radial
            real = summed_ref[b, at + radial : at + 2 * radial] * scale
            imag = summed_ref[b, at : at + radial] * (-scale)
            for part, value in ((0, real), (1, imag)):
                if not last:
                    next_refs[k][b, 0, part] = value
                if not sums_in:
                    continue
                value = sum_refs[k][b, 0, part] + value
                if not last:
                    value = term_refs[k][b, 0, part] + value
                    total_refs[k][b, 0, part] = value
                else:
                    out_ref[k, b, 0, part] = value


def taylor(degree, terms, halo, sums, tile_list, tiles, weights, window, factor, afters):
    helices = window.shape[0] - 1
    last = degree == TAYLOR
    shape = (halo.shape[0], *halo.shape[2:]) if isinstance(halo, jax.Array) else halo[0].shape
    blocks, count, parts, radial, lanes = shape
    block = pl.BlockSpec((blocks, 1, parts, ROWS, lanes), lambda v, j, lists: (0, v, 0, j, 0))

    def whole(array):
        zeros = (0,) * array.ndim
        return pl.BlockSpec(
            array.shape, lambda v, j, lists: zeros, pipeline_mode=pl.Buffered(1)
        )

    def helix(k):
        return pl.BlockSpec(
            (blocks, 1, 1, parts, ROWS, lanes), lambda v, j, lists: (0, k, v, 0, j, 0)
        )

    def per_helix(fields):
        if isinstance(fields, (list, tuple)):
            return list(fields), [block] * len(fields)
        held = fields.shape[1]
        return [fields] * held, [helix(k) for k in range(held)]

    own, own_specs = per_helix(terms)
    sides, side_specs = per_helix(halo)
    operands = [*afters, *own, *sides, tiles, weights, window, factor]
    specs = [*[ANYWHERE] * len(afters), *own_specs, *side_specs]
    specs += [
        whole(tiles),
        pl.BlockSpec((weights.shape[0], ROWS, lanes), lambda v, j, lists: (0, j, 0)),
        whole(window),
        pl.BlockSpec((ROWS, lanes), lambda v, j, lists: (j, 0)),
    ]
    if sums is not None:
        summed, summed_specs = per_helix(sums)
        operands += summed
        specs += summed_specs
    field = jax.ShapeDtypeStruct(shape, jnp.float32)
    if last:
        shapes = [jax.ShapeDtypeStruct((helices, *shape), jnp.float32)]
        out_specs = [
            pl.BlockSpec(
                (helices, blocks, 1, parts, ROWS, lanes),
                lambda v, j, lists: (0, 0, v, 0, j, 0),
            )
        ]
    else:
        written = helices if sums is None else 2 * helices
        shapes = [field] * written
        out_specs = [block] * written
    rows = helices * parts * ROWS
    results = pl.pallas_call(
        functools.partial(
            taylor_kernel, degree, helices, len(afters), sums is not None, last
        ),
        grid_spec=pltpu.PrefetchScalarGridSpec(
            num_scalar_prefetch=1,
            grid=(count, radial // ROWS),
            in_specs=specs,
            out_specs=out_specs,
            scratch_shapes=[
                pltpu.VMEM((blocks, rows, 2 * lanes), jnp.bfloat16),
                pltpu.VMEM((blocks, rows, lanes), jnp.float32),
            ],
        ),
        out_shape=shapes,
        compiler_params=params(2),
        cost_estimate=pl.CostEstimate(
            flops=2 * 4 * count * helices * parts * radial * lanes * lanes * tiles.shape[0],
            bytes_accessed=4 * blocks * count * parts * radial * lanes * (helices + 2 + 2 * helices),
            transcendentals=0,
        ),
    )(tile_list, *operands)
    if last:
        return results[0], None
    return results[:helices], terms if sums is None else results[helices:]


def body_blocks(packet, radial_weight, tile_blocks, tile_list, coupling):
    _, helices, radial, _, channels = packet.shape
    blocks = channels // TILE
    count = lax.axis_size("hel")
    forward = [(i, i + 1) for i in range(count - 1)]
    backward = [(target, source) for source, target in forward]
    exchange = functools.partial(
        lax.all_to_all, axis_name="rad", split_axis=0, concat_axis=0, tiled=True
    )

    length = blocks * radial
    packed = pack(packet, [0])
    packed += pack(packet, list(range(1, len(CHUNKS))))
    high, low = circulant(length, 2 * radial)
    tile_high = lax.reduce_precision(tile_blocks, 8, 7)
    tile_low = (tile_blocks - tile_high).astype(jnp.bfloat16)
    tile_high = tile_high.astype(jnp.bfloat16)
    pair = jnp.concatenate([tile_high, tile_low], axis=2)
    tiles = jnp.concatenate([pair, pair], axis=1)
    weights = jnp.broadcast_to(radial_weight[:, :, None], (*radial_weight.shape, TILE))
    window = coupling_window(coupling, helices).reshape(helices + 1, blocks, 1, TILE)
    factor = jnp.broadcast_to(radial_factor_of(radial)[:, None], (radial, TILE))

    spectra, terms, halos, sums, degrees = {}, {}, {}, {}, {}
    previous, latest = (), ()

    def send(value):
        nonlocal previous, latest
        afters = [a for a in (*previous, *latest) if a is not value]
        if afters:
            value = gate(value, *afters)
            latest = (value,)
        previous = (exchange(value),)
        return previous[0]

    def halo(c, degree, first, last):
        degrees[c] = degree
        below = lax.ppermute(last, "hel", forward)
        halos[c] = below, lax.ppermute(first, "hel", backward)

    for c in EARLY:
        halo(c, 0, packed[c][:, 0], packed[c][:, -1])

    def run(kind, c):
        nonlocal latest
        if kind == "F":
            spectra[c] = send(packed[c])
        elif kind == "K":
            spectra[c] = kinetic(spectra[c], high, low, latest)
            latest = (spectra[c],)
        elif kind == "B":
            terms[c] = send(spectra[c])
        elif kind == "G":
            halos[c] = send(jnp.stack(halos[c], axis=1))
        elif kind == "L":
            halos[c] = kinetic(halos[c], high, low, latest)
            latest = (halos[c],)
        elif kind == "C":
            halos[c] = send(halos[c])
            degrees[c] = 1
        elif kind == "T":
            degree = degrees[c]
            terms[c], sums[c] = taylor(
                degree,
                terms[c],
                halos[c],
                sums.get(c),
                tile_list,
                tiles,
                weights,
                window,
                factor,
                latest,
            )
            latest = (terms[c],) if degree == TAYLOR else (terms[c][0],)

    for kind, c in PLAN:
        run(kind, c)
        if kind == "E":
            latest = terms[c][:, 0], terms[c][:, -1]
            halo(c, 1, *latest)
        elif kind == "T" and degrees[c] < TAYLOR:
            halo(c, degrees[c] + 1, terms[c][0], terms[c][-1])
    return unpack([terms[c] for c in range(len(CHUNKS))], packet.shape)


def solution(mesh):
    in_specs = (P(None, "hel", "rad", None, None), P(None, "rad"), P(), P(), P())
    out_specs = P(None, "hel", "rad", None, None)

    def sharded(body):
        return jax.shard_map(
            body, mesh=mesh, in_specs=in_specs, out_specs=out_specs, check_vma=False
        )

    def step(packet, *others):
        _, _, points, vibration, channels = packet.shape
        whole_blocks = channels == mesh.shape["rad"] * TILE
        whole_rows = points == mesh.shape["rad"] * TILE and vibration == sum(CHUNKS)
        if not (whole_blocks and whole_rows):
            return sharded(body_any)(packet, *others)

        return sharded(body_blocks)(packet, *others)

    return step
```

```python
import functools

import jax
import jax.numpy as jnp
import numpy as np
from jax import lax
from jax.experimental import pallas as pl
from jax.experimental.pallas import tpu as pltpu
from jax.sharding import PartitionSpec as P


R = 1024
TILE = 128
TAYLOR = 3
CHUNKS = (2, 1, 2, 2, 1)
EARLY = (4,)
PLAN = (
    ("F", 0), ("F", 1), ("K", 0), ("B", 0), ("K", 1), ("E", 0), ("B", 1), ("F", 2), ("E", 1),
    ("T", 0), ("K", 2), ("B", 2), ("T", 1), ("T", 0), ("F", 3), ("E", 2), ("T", 1), ("F", 4),
    ("K", 3), ("B", 3), ("T", 2), ("T", 1), ("K", 4), ("B", 4), ("E", 3), ("T", 2), ("G", 4),
    ("T", 3), ("L", 4), ("C", 4), ("T", 0), ("T", 2), ("T", 4), ("T", 3), ("T", 4), ("T", 3),
    ("T", 4),
)


kinetic_scale = 0.5


def extended(block, sides, width):
    for axis, dim in sides:
        count = lax.axis_size(axis)
        forward = [(i, i + 1) for i in range(count - 1)]
        backward = [(target, source) for source, target in forward]
        low = lax.ppermute(
            lax.slice_in_dim(block, block.shape[dim] - width, None, axis=dim), axis, forward
        )
        high = lax.ppermute(lax.slice_in_dim(block, 0, width, axis=dim), axis, backward)
        block = jnp.concatenate([low, block, high], axis=dim)
    return block


def potential(term, radial_weight, tile_blocks, tile_list):
    term_shape = term.shape
    blocks = term.reshape(
        term_shape[0], term_shape[1], term_shape[2], term_shape[3], term_shape[4] // TILE, TILE
    )

    def add_tile(position, summed):
        target = tile_list[position, 0]
        source = tile_list[position, 1]
        weight_row = tile_list[position, 2]
        source_block = lax.dynamic_index_in_dim(blocks, source, 4, keepdims=False)
        matrix = lax.dynamic_index_in_dim(tile_blocks, position, 0, keepdims=False)
        product = jnp.einsum(
            "ckrvi,ij->ckrvj", source_block, matrix, precision=lax.Precision.HIGHEST
        )
        factor = lax.dynamic_index_in_dim(radial_weight, weight_row, 0, keepdims=False)
        product = product * factor[None, None, :, None, None]
        current = lax.dynamic_index_in_dim(summed, target, 4, keepdims=False)
        return lax.dynamic_update_index_in_dim(summed, current + product, target, 4)

    summed = lax.fori_loop(0, tile_list.shape[0], add_tile, jnp.zeros(blocks.shape, jnp.float32))
    return summed.reshape(term_shape)


def coupling_window(coupling, helices):
    first_helix = lax.axis_index("hel") * helices
    coupled = jnp.concatenate([jnp.zeros((1, coupling.shape[1]), jnp.float32), coupling], axis=0)
    return lax.dynamic_slice_in_dim(coupled, first_helix, helices + 1, 0)


def coriolis_rim(term, coupling, radial_factor):
    helices = term.shape[1]
    padded = extended(term, (("hel", 1),), 1)
    window = coupling_window(coupling, helices)
    lower = window[:helices]
    upper = window[1:]
    mixed = (
        upper[None, :, None, None, :] * padded[:, 2:]
        + lower[None, :, None, None, :] * padded[:, :-2]
    )
    return mixed * radial_factor[None, None, :, None, None]


def transform(matrix, moving):
    return jnp.einsum("qr,cnrm->cnqm", matrix, moving, precision=lax.Precision.HIGHEST)


def propagate(moving, cosine_table, sine_table, phase_cos, phase_sin):
    length = moving.shape[2]
    cos_part = transform(cosine_table, moving)
    sin_part = transform(sine_table, moving)
    spec_real = cos_part[0] + sin_part[1]
    spec_imag = cos_part[1] - sin_part[0]
    turn_cos = phase_cos[None, :, None]
    turn_sin = phase_sin[None, :, None]
    turned = jnp.stack(
        [turn_cos * spec_real + turn_sin * spec_imag, turn_cos * spec_imag - turn_sin * spec_real]
    )
    cos_back = transform(cosine_table, turned)
    sin_back = transform(sine_table, turned)
    return jnp.stack([(cos_back[0] - sin_back[1]) / length, (cos_back[1] + sin_back[0]) / length])


def expand(current, radial_weight, tile_blocks, tile_list, coupling, radial_factor, coriolis):
    advanced = current
    for degree in range(1, TAYLOR + 1):
        applied = potential(current, radial_weight, tile_blocks, tile_list) + coriolis(
            current, coupling, radial_factor
        )
        current = jnp.stack([applied[1], -applied[0]]) / degree
        advanced = advanced + current
    return advanced


def radial_factor_of(radial):
    distance = (lax.axis_index("rad") * radial + jnp.arange(radial, dtype=jnp.int32)).astype(
        jnp.float32
    )
    return 1.0 / (1.0 + 3.0 * distance / R) ** 2


def body_any(packet, radial_weight, tile_blocks, tile_list, coupling):
    two_parts, helices, radial, vibration, channels = packet.shape
    wave_index = jnp.arange(R, dtype=jnp.int32)
    angle_table = (wave_index[:, None] * wave_index[None, :] % R).astype(jnp.float32) * (
        2.0 * jnp.pi / R
    )
    cosine_table = jnp.cos(angle_table)
    sine_table = jnp.sin(angle_table)
    signed = jnp.where(wave_index < R // 2, wave_index, wave_index - R).astype(jnp.float32)
    phase_angle = kinetic_scale * (2.0 * jnp.pi * signed / R) ** 2
    phase_cos = jnp.cos(phase_angle)
    phase_sin = jnp.sin(phase_angle)
    flattened = packet.reshape(two_parts, helices, radial, vibration * channels)
    moved = propagate(
        lax.all_to_all(flattened, "rad", split_axis=3, concat_axis=2, tiled=True),
        cosine_table,
        sine_table,
        phase_cos,
        phase_sin,
    )
    returned = lax.all_to_all(moved, "rad", split_axis=2, concat_axis=3, tiled=True)
    current = returned.reshape(packet.shape)
    return expand(
        current,
        radial_weight,
        tile_blocks,
        tile_list,
        coupling,
        radial_factor_of(radial),
        coriolis_rim,
    )


VMEM_LIMIT = 60 * 1024 * 1024


def params(axes):
    return pltpu.CompilerParams(
        dimension_semantics=("arbitrary",) * axes, vmem_limit_bytes=VMEM_LIMIT
    )


def split_two(value):
    high = value.astype(jnp.bfloat16)
    low = (value - high.astype(jnp.float32)).astype(jnp.bfloat16)
    return high, low


def propagator_column(length):
    wave = np.arange(length)
    signed = np.where(wave < length // 2, wave, wave - length).astype(np.float64)
    phase = kinetic_scale * (2.0 * np.pi * signed / length) ** 2
    column = np.fft.ifft(np.exp(-1j * phase))
    return column.real.astype(np.float32), column.imag.astype(np.float32)


STRIPE = 16
ROWS = 64
UNROLL = 8


def circulant_kernel(real_ref, imag_ref, high_ref, low_ref):
    rows = high_ref.shape[2]
    first = pl.program_id(0) * rows
    for part, ref in ((0, real_ref), (1, imag_ref)):
        stripe = jnp.broadcast_to(ref[...], (STRIPE, ref.shape[1]))
        row = lax.broadcasted_iota(jnp.int32, stripe.shape, 0)
        step = 1
        while step < STRIPE:
            stripe = jnp.where(row // step % 2 == 1, pltpu.roll(stripe, step, 1), stripe)
            step *= 2

        @pl.loop(0, rows // STRIPE)
        def _(j):
            at = pl.multiple_of(j * STRIPE, STRIPE)
            high, low = split_two(pltpu.roll(stripe, first + at, 1))
            high_ref[0, part, pl.ds(at, STRIPE)] = high
            low_ref[0, part, pl.ds(at, STRIPE)] = low


def circulant(length, rows):
    real, imag = propagator_column(length)
    grid = length // rows
    spec = pl.BlockSpec((1, 2, rows, length), lambda m: (m, 0, 0, 0))
    line = pl.BlockSpec((1, length), lambda m: (0, 0))
    shape = jax.ShapeDtypeStruct((grid, 2, rows, length), jnp.bfloat16)
    return pl.pallas_call(
        circulant_kernel,
        grid=(grid,),
        in_specs=[line, line],
        out_specs=[spec, spec],
        out_shape=[shape, shape],
        compiler_params=params(1),
        name="circulant",
    )(jnp.asarray(real)[None], jnp.asarray(imag)[None])


def kinetic_kernel(*refs):
    moving_ref, high_ref, low_ref, out_ref, xh_ref, xl_ref = refs[-6:]
    sources, _, _, _, radial, lanes = moving_ref.shape
    length = sources * radial
    for part in range(2):
        value = moving_ref[:, 0, 0, part].reshape(length, lanes)
        high, low = split_two(value)
        xh_ref[:, part * lanes : (part + 1) * lanes] = high
        xl_ref[:, part * lanes : (part + 1) * lanes] = low
    groups, _, rows, _ = high_ref.shape
    per = rows // radial

    @pl.loop(0, groups, unroll=2)
    def _(m):
        left = high_ref[m].reshape(2 * rows, length)
        small = low_ref[m].reshape(2 * rows, length)
        dot = functools.partial(jnp.dot, preferred_element_type=jnp.float32)
        high = xh_ref[...]
        total = dot(left, high) + (dot(left, xl_ref[...]) + dot(small, high))
        real = total[:rows, :lanes] - total[rows:, lanes:]
        imag = total[:rows, lanes:] + total[rows:, :lanes]
        for j in range(per):
            out_ref[m * per + j, 0, 0, 0] = real[j * radial : (j + 1) * radial]
            out_ref[m * per + j, 0, 0, 1] = imag[j * radial : (j + 1) * radial]


def kinetic(moving, high, low, afters):
    blocks, helices, count, _, radial, lanes = moving.shape
    block = pl.BlockSpec((blocks, 1, 1, 2, radial, lanes), lambda k, v: (0, k, v, 0, 0, 0))
    whole = pl.BlockSpec(high.shape, lambda k, v: (0, 0, 0, 0), pipeline_mode=pl.Buffered(1))
    length = blocks * radial
    return pl.pallas_call(
        kinetic_kernel,
        grid=(helices, count),
        in_specs=[*[ANYWHERE] * len(afters), block, whole, whole],
        out_specs=block,
        out_shape=jax.ShapeDtypeStruct(moving.shape, jnp.float32),
        scratch_shapes=[
            pltpu.VMEM((length, 2 * lanes), jnp.bfloat16),
            pltpu.VMEM((length, 2 * lanes), jnp.bfloat16),
        ],
        compiler_params=params(2),
        cost_estimate=pl.CostEstimate(
            flops=2 * 3 * helices * count * 4 * length * length * lanes,
            bytes_accessed=8 * moving.size + 8 * length * length,
            transcendentals=0,
        ),
        name="kinetic",
    )(*afters, moving, high, low)


def places():
    return [(c, i) for c, count in enumerate(CHUNKS) for i in range(count)]


def pack_kernel(chunks, packet_ref, *chunk_refs):
    @pl.loop(0, packet_ref.shape[4] // TILE)
    def _(b):
        lanes = pl.ds(pl.multiple_of(b * TILE, TILE), TILE)
        turned = jnp.swapaxes(packet_ref[0, 0, :, :, lanes], 0, 1)
        for v, (c, i) in enumerate(places()):
            if c in chunks:
                chunk_refs[chunks.index(c)][b, 0, i, 0] = turned[v]


def pack(packet, chunks):
    parts, helices, radial, vibration, channels = packet.shape
    blocks = channels // TILE
    counts = [CHUNKS[c] for c in chunks]
    share = sum(counts) / vibration
    return pl.pallas_call(
        functools.partial(pack_kernel, chunks),
        grid=(helices, parts),
        in_specs=[
            pl.BlockSpec((1, 1, radial, vibration, channels), lambda k, p: (p, k, 0, 0, 0))
        ],
        out_specs=[
            pl.BlockSpec((blocks, 1, count, 1, radial, TILE), lambda k, p: (0, k, 0, p, 0, 0))
            for count in counts
        ],
        out_shape=[
            jax.ShapeDtypeStruct((blocks, helices, count, parts, radial, TILE), jnp.float32)
            for count in counts
        ],
        compiler_params=params(2),
        cost_estimate=pl.CostEstimate(
            flops=0, bytes_accessed=int(4 * packet.size * (1 + share)), transcendentals=0
        ),
        name="pack",
    )(packet)


def unpack_kernel(*refs):
    out_ref = refs[-1]

    @pl.loop(0, out_ref.shape[4] // TILE)
    def _(b):
        lanes = pl.ds(pl.multiple_of(b * TILE, TILE), TILE)
        lines = [refs[c][0, b, i, 0] for c, i in places()]
        out_ref[0, 0, :, :, lanes] = jnp.swapaxes(jnp.stack(lines), 0, 1)


def unpack(chunks, packet_shape):
    parts, helices, radial, vibration, channels = packet_shape
    blocks = channels // TILE
    return pl.pallas_call(
        unpack_kernel,
        grid=(helices, parts),
        in_specs=[
            pl.BlockSpec((1, blocks, count, 1, radial, TILE), lambda k, p: (k, 0, 0, p, 0, 0))
            for count in CHUNKS
        ],
        out_specs=pl.BlockSpec(
            (1, 1, radial, vibration, channels), lambda k, p: (p, k, 0, 0, 0)
        ),
        out_shape=jax.ShapeDtypeStruct(packet_shape, jnp.float32),
        compiler_params=params(2),
        name="unpack",
    )(*chunks)


def gate_kernel(*refs):
    del refs


ANYWHERE = pl.BlockSpec(memory_space=pl.ANY)


def gate(value, *afters):
    return pl.pallas_call(
        gate_kernel,
        in_specs=[ANYWHERE] * (1 + len(afters)),
        out_specs=ANYWHERE,
        out_shape=jax.ShapeDtypeStruct(value.shape, value.dtype),
        input_output_aliases={0: 0},
        compiler_params=params(0),
        name="gate",
    )(value, *afters)


def taylor_kernel(degree, helices, skipped, sums_in, last, list_ref, *refs):
    refs = list(refs)[skipped:]
    term_refs = [refs.pop(0) for _ in range(helices)]
    low_ref, high_ref, tile_ref, weight_ref, window_ref, factor_ref = (
        refs.pop(0) for _ in range(6)
    )
    sum_refs = [refs.pop(0) for _ in range(helices)] if sums_in else []
    next_refs = None if last else [refs.pop(0) for _ in range(helices)]
    total_refs = [refs.pop(0) for _ in range(helices)] if sums_in and not last else None
    out_ref = refs.pop(0) if last else None
    split_ref, summed_ref = refs
    term_refs, sum_refs, (low_ref, high_ref) = (
        [r.at[:, 0] if len(r.shape) == 6 else r for r in some]
        for some in (term_refs, sum_refs, (low_ref, high_ref))
    )
    blocks, _, _, radial, lanes = term_refs[0].shape
    rows = helices * 2 * radial
    factor = factor_ref[...]

    @pl.loop(0, blocks)
    def _(b):
        for k in range(helices):
            below = low_ref if k == 0 else term_refs[k - 1]
            above = high_ref if k == helices - 1 else term_refs[k + 1]
            lower = window_ref[k, b]
            upper = window_ref[k + 1, b]
            for part in range(2):
                at = (k * 2 + part) * radial
                high, low = split_two(term_refs[k][b, 0, part])
                split_ref[b, at : at + radial, :lanes] = high
                split_ref[b, at : at + radial, lanes:] = low
                mixed = upper * above[b, 0, part] + lower * below[b, 0, part]
                summed_ref[b, at : at + radial] = mixed * factor

    def add_tile(t, carry):
        target = list_ref[t, 0]
        source = list_ref[t, 1]
        weight = weight_ref[list_ref[t, 2]]
        both = jnp.dot(split_ref[source], tile_ref[t], preferred_element_type=jnp.float32)
        for i in range(rows // radial):
            at = i * radial
            product = both[at : at + radial, :lanes] + both[at : at + radial, lanes:]
            summed_ref[target, at : at + radial] += product * weight
        return carry

    lax.fori_loop(0, tile_ref.shape[0], add_tile, 0, unroll=UNROLL)

    scale = 1.0 / degree

    @pl.loop(0, blocks)
    def _(b):
        for k in range(helices):
            at = k * 2 * radial
            real = summed_ref[b, at + radial : at + 2 * radial] * scale
            imag = summed_ref[b, at : at + radial] * (-scale)
            for part, value in ((0, real), (1, imag)):
                if not last:
                    next_refs[k][b, 0, part] = value
                if not sums_in:
                    continue
                value = sum_refs[k][b, 0, part] + value
                if not last:
                    value = term_refs[k][b, 0, part] + value
                    total_refs[k][b, 0, part] = value
                else:
                    out_ref[k, b, 0, part] = value


def taylor(degree, terms, halo, sums, tile_list, tiles, weights, window, factor, afters):
    helices = window.shape[0] - 1
    last = degree == TAYLOR
    shape = (halo.shape[0], *halo.shape[2:]) if isinstance(halo, jax.Array) else halo[0].shape
    blocks, count, parts, radial, lanes = shape
    block = pl.BlockSpec((blocks, 1, parts, ROWS, lanes), lambda v, j, lists: (0, v, 0, j, 0))

    def whole(array):
        zeros = (0,) * array.ndim
        return pl.BlockSpec(
            array.shape, lambda v, j, lists: zeros, pipeline_mode=pl.Buffered(1)
        )

    def helix(k):
        return pl.BlockSpec(
            (blocks, 1, 1, parts, ROWS, lanes), lambda v, j, lists: (0, k, v, 0, j, 0)
        )

    def per_helix(fields):
        if isinstance(fields, (list, tuple)):
            return list(fields), [block] * len(fields)
        held = fields.shape[1]
        return [fields] * held, [helix(k) for k in range(held)]

    own, own_specs = per_helix(terms)
    sides, side_specs = per_helix(halo)
    operands = [*afters, *own, *sides, tiles, weights, window, factor]
    specs = [*[ANYWHERE] * len(afters), *own_specs, *side_specs]
    specs += [
        whole(tiles),
        pl.BlockSpec((weights.shape[0], ROWS, lanes), lambda v, j, lists: (0, j, 0)),
        whole(window),
        pl.BlockSpec((ROWS, lanes), lambda v, j, lists: (j, 0)),
    ]
    if sums is not None:
        summed, summed_specs = per_helix(sums)
        operands += summed
        specs += summed_specs
    field = jax.ShapeDtypeStruct(shape, jnp.float32)
    if last:
        shapes = [jax.ShapeDtypeStruct((helices, *shape), jnp.float32)]
        out_specs = [
            pl.BlockSpec(
                (helices, blocks, 1, parts, ROWS, lanes),
                lambda v, j, lists: (0, 0, v, 0, j, 0),
            )
        ]
    else:
        written = helices if sums is None else 2 * helices
        shapes = [field] * written
        out_specs = [block] * written
    rows = helices * parts * ROWS
    results = pl.pallas_call(
        functools.partial(
            taylor_kernel, degree, helices, len(afters), sums is not None, last
        ),
        grid_spec=pltpu.PrefetchScalarGridSpec(
            num_scalar_prefetch=1,
            grid=(count, radial // ROWS),
            in_specs=specs,
            out_specs=out_specs,
            scratch_shapes=[
                pltpu.VMEM((blocks, rows, 2 * lanes), jnp.bfloat16),
                pltpu.VMEM((blocks, rows, lanes), jnp.float32),
            ],
        ),
        out_shape=shapes,
        compiler_params=params(2),
        cost_estimate=pl.CostEstimate(
            flops=2 * 4 * count * helices * parts * radial * lanes * lanes * tiles.shape[0],
            bytes_accessed=4 * blocks * count * parts * radial * lanes * (helices + 2 + 2 * helices),
            transcendentals=0,
        ),
    )(tile_list, *operands)
    if last:
        return results[0], None
    return results[:helices], terms if sums is None else results[helices:]


def body_blocks(packet, radial_weight, tile_blocks, tile_list, coupling):
    _, helices, radial, _, channels = packet.shape
    blocks = channels // TILE
    count = lax.axis_size("hel")
    forward = [(i, i + 1) for i in range(count - 1)]
    backward = [(target, source) for source, target in forward]
    exchange = functools.partial(
        lax.all_to_all, axis_name="rad", split_axis=0, concat_axis=0, tiled=True
    )

    length = blocks * radial
    packed = pack(packet, [0])
    packed += pack(packet, list(range(1, len(CHUNKS))))
    high, low = circulant(length, 2 * radial)
    tile_high = lax.reduce_precision(tile_blocks, 8, 7)
    tile_low = (tile_blocks - tile_high).astype(jnp.bfloat16)
    tile_high = tile_high.astype(jnp.bfloat16)
    pair = jnp.concatenate([tile_high, tile_low], axis=2)
    tiles = jnp.concatenate([pair, pair], axis=1)
    weights = jnp.broadcast_to(radial_weight[:, :, None], (*radial_weight.shape, TILE))
    window = coupling_window(coupling, helices).reshape(helices + 1, blocks, 1, TILE)
    factor = jnp.broadcast_to(radial_factor_of(radial)[:, None], (radial, TILE))

    spectra, terms, halos, sums, degrees = {}, {}, {}, {}, {}
    previous = ()

    def send(value):
        nonlocal previous, latest
        if previous:
            afters = [a for a in (*previous, *latest) if a is not value]
            value = gate(value, *afters)
            latest = (value,)
        previous = (exchange(value),)
        return previous[0]

    def halo(c, degree, first, last):
        degrees[c] = degree
        below = lax.ppermute(last, "hel", forward)
        halos[c] = below, lax.ppermute(first, "hel", backward)

    latest = (high,)
    for c in EARLY:
        latest += packed[c][:, 0], packed[c][:, -1]
        halo(c, 0, *latest[-2:])

    def run(kind, c):
        nonlocal latest
        if kind == "F":
            spectra[c] = send(packed[c])
        elif kind == "K":
            spectra[c] = kinetic(spectra[c], high, low, latest)
            latest = (spectra[c],)
        elif kind == "B":
            terms[c] = send(spectra[c])
        elif kind == "G":
            halos[c] = send(jnp.stack(halos[c], axis=1))
        elif kind == "L":
            halos[c] = kinetic(halos[c], high, low, latest)
            latest = (halos[c],)
        elif kind == "C":
            halos[c] = send(halos[c])
            degrees[c] = 1
        elif kind == "T":
            degree = degrees[c]
            terms[c], sums[c] = taylor(
                degree,
                terms[c],
                halos[c],
                sums.get(c),
                tile_list,
                tiles,
                weights,
                window,
                factor,
                latest,
            )
            latest = (terms[c],) if degree == TAYLOR else (terms[c][0],)

    for kind, c in PLAN:
        run(kind, c)
        if kind == "E":
            latest = terms[c][:, 0], terms[c][:, -1]
            halo(c, 1, *latest)
        elif kind == "T" and degrees[c] < TAYLOR:
            halo(c, degrees[c] + 1, terms[c][0], terms[c][-1])
    return unpack([terms[c] for c in range(len(CHUNKS))], packet.shape)


def solution(mesh):
    in_specs = (P(None, "hel", "rad", None, None), P(None, "rad"), P(), P(), P())
    out_specs = P(None, "hel", "rad", None, None)

    def sharded(body):
        return jax.shard_map(
            body, mesh=mesh, in_specs=in_specs, out_specs=out_specs, check_vma=False
        )

    def step(packet, *others):
        _, _, points, vibration, channels = packet.shape
        whole_blocks = channels == mesh.shape["rad"] * TILE
        whole_rows = points == mesh.shape["rad"] * TILE and vibration == sum(CHUNKS)
        if not (whole_blocks and whole_rows):
            return sharded(body_any)(packet, *others)

        return sharded(body_blocks)(packet, *others)

    return step
```
